256 devices in a mesh: term: 16 (over y_lo, z), sector: 16 (over y_hi, x, core).
Axes of the slice: x: 4, y: 4 (y_hi: 2, y_lo: 2; y = y_hi * 2 + y_lo), z: 8, core: 2. Of those that a mesh axis runs over, the one named last changes fastest.
Arguments:
- wavefunction: bfloat16 [4096, 128, 128], P(('term', 'sector')), may hold values from -6 to 6
- left_sector: int32 [4096, 1], P(('term', 'sector')), may hold values from 0 to 15; in each aligned block of 16 rows (0 to 15, 16 to 31, ...) at most 2 rows name the same one
- right_sector: int32 [4096], P(('term', 'sector')), may hold values from 0 to 3
- left_blocks: bfloat16 [32, 16, 128, 128], P('term', 'sector'), may hold values from -0.5 to 0.5
- right_blocks: bfloat16 [32, 4, 128, 128], P('term'), may hold values from -0.09375 to 0.09375
Outputs:
- product_blocks: bfloat16 [4096, 128, 128], P(('term', 'sector'))
The draws below stay inside these ranges and needn't reach their ends.
Inputs may be any that keep to these rules, and one draw needn't show every extreme that they name: `left_sector`: among the 16 blocks of one device no left sector is named more than 2 times, and some left sector is named exactly 2 times.
All inputs are finite; a program needn't handle non-finite values.
Results may differ from the reference program's by a relative error of at most 0.0049.
Values may be sent and summed in bfloat16 or wider, within the bound.
A program may use at most 64 MiB of HBM per device.

```python
import math
import jax
import jax.numpy as jnp
import numpy as np
from jax import lax

BLOCK = 128
BLK_DEV = 16
TERM_DEV = 2
RSEC = 4
CAP = 2
TERMS = 32
NBLK = 4096
N_TERM = 16
N_SECTOR = 16


def set_ends(result, rng, least, largest):
    shape = result.shape
    index_at = [jax.random.randint(jax.random.fold_in(rng, axis), (), 0, shape[axis]) for axis in range(len(shape))]
    result = result.at[tuple(index_at)].set(least)
    longest = shape.index(max(shape))
    index_at[longest] = (index_at[longest] + 1) % shape[longest]
    return result.at[tuple(index_at)].set(largest)


def block_scale(rng, shape, split, least, top_value):
    factor_of, own = 1.0, jax.random.fold_in(rng, 6)
    for position, blocks in split:
        heights = jnp.exp(jax.random.uniform(jax.random.fold_in(own, position), (blocks,), jnp.float32, least / len(split), top_value / len(split)))
        factor_of = factor_of * jnp.repeat(heights, shape[position] // blocks).reshape([-1 if axis == position else 1 for axis in range(len(shape))])
    return factor_of


def deal_out(own_key, own, number, rows, amount, top, limit, skew):
    sequence = jax.random.permutation(own_key, amount)
    crowded, ordinary = portions_of(amount, rows * top, limit, skew, True), portions_of(amount, rows * top, limit, skew, False)
    places = jnp.arange(amount)

    def named(lengths, rotation):
        used = int((lengths > 0).sum())
        fixed = max(1, used // 4)
        passed = fixed + (places - fixed + rotation * (used - fixed)) % max(1, amount - fixed)
        return jnp.zeros((amount,), jnp.int32).at[sequence[jnp.where(places < fixed, places, passed)]].set(jnp.asarray(lengths, jnp.int32))

    lengths = jnp.where(number % 4 == 0, named(crowded, number // 4), named(ordinary, number - number // 4 - 1))
    mixed = jax.random.permutation(jax.random.fold_in(own, 3), amount)
    source_of, sink = mixed[0:amount // 2 * 2:2], mixed[1:amount // 2 * 2:2]
    margin = jnp.minimum(lengths[source_of] - 1, limit - lengths[sink]) // 2
    margin = jnp.where((source_of == sequence[0]) | (sink == sequence[0]) | (lengths[sink] == 0), 0, jnp.maximum(margin, 0))
    passed = jax.random.randint(jax.random.fold_in(own, 4), (amount // 2,), 0, 1 << 20) % (margin + 1)
    lengths = lengths.at[source_of].add(-passed).at[sink].add(passed)
    members = jnp.searchsorted(jnp.cumsum(lengths), jnp.arange(rows * top), side="right").astype(jnp.int32)
    table = members.reshape(top, rows).T
    table = table[jax.random.permutation(jax.random.fold_in(own, 1), rows)]
    rotation = jax.random.randint(jax.random.fold_in(own, 2), (rows, 1), 0, top)
    return jnp.take_along_axis(table, (jnp.arange(top)[None, :] + rotation) % top, axis=1)


def portions_of(count, total, bound, slope, full):
    loads = [(1 << 20) // math.isqrt(standing ** slope) + 1 for standing in range(1, count + 1)]
    largest = bound if full else min(bound, max(-(-total // count), total * loads[0] // sum(loads)))
    least = 1 if total - largest >= count - 1 else 0
    holding, spare = [largest] + [least] * (count - 1), total - largest - least * (count - 1)
    while spare > 0:
        candidates = [i for i in range(1, count) if holding[i] < largest] or [i for i in range(1, count) if holding[i] < bound]
        whole, budget = sum([loads[i] for i in candidates]), spare
        for i in candidates:
            addition = min(bound - holding[i], max(1, budget * loads[i] // whole), spare)
            holding[i] = holding[i] + addition
            spare = spare - addition
    return np.array(holding)


def noise(key, extent, deviation, limit, split=(), held_as=jnp.bfloat16):
    entries = deviation * jax.random.normal(key, extent, jnp.float32)
    if split:
        entries = entries * block_scale(key, extent, split, -0.22, 0.18)
    return jnp.clip(entries, -limit, limit).astype(held_as)


def setup_inputs(seed: int = 0) -> dict:
    keys = jax.random.split(jax.random.key(seed), 6)
    wavefunction = noise(keys[0], (NBLK, BLOCK, BLOCK), 1.0, 6.0, ((0, 256),))
    left_sector_keys = jax.random.split(jax.random.fold_in(keys[1], 1), NBLK // BLK_DEV)
    left_sector_turns = jax.random.permutation(jax.random.fold_in(keys[1], 3), NBLK // BLK_DEV)
    left_sector = jax.vmap(lambda own, number: deal_out(jax.random.fold_in(keys[1], 2), own, number, BLK_DEV, N_SECTOR, 1, CAP, 2))(left_sector_keys, left_sector_turns).reshape((NBLK, 1))
    right_sector = set_ends(jax.random.randint(keys[2], (NBLK,), 0, RSEC), jax.random.fold_in(keys[2], 1), 0, RSEC - 1).astype(jnp.int32)
    left_blocks = noise(keys[3], (TERMS, N_SECTOR, BLOCK, BLOCK), BLOCK ** -0.5, 0.5, ((0, 16), (1, 16)))
    right_blocks = noise(keys[4], (TERMS, RSEC, BLOCK, BLOCK), (BLOCK * TERM_DEV * N_TERM) ** -0.5, 0.09375, ((0, 16),))
    return {"wavefunction": wavefunction, "left_sector": left_sector, "right_sector": right_sector, "left_blocks": left_blocks, "right_blocks": right_blocks}


def reference(wavefunction, left_sector, right_sector, left_blocks, right_blocks):
    left_of = left_sector[:, 0].astype(jnp.int32)
    wave_wide = wavefunction.astype(jnp.float32)

    def add_term(summed, index_term):
        left_here = jnp.take(left_blocks[index_term], left_of, axis=0).astype(jnp.float32)
        mixed_left = jnp.einsum("kab,kbc->kac", left_here, wave_wide).astype(jnp.bfloat16)
        right_here = jnp.take(right_blocks[index_term], right_sector, axis=0).astype(jnp.float32)
        return summed + jnp.einsum("kac,kdc->kad", mixed_left.astype(jnp.float32), right_here), None

    summed, _ = lax.scan(add_term, jnp.zeros(wavefunction.shape, jnp.float32), jnp.arange(TERMS, dtype=jnp.int32))
    return summed.astype(jnp.bfloat16)
```

```python
import functools

import jax
import jax.numpy as jnp
from jax import lax
from jax.experimental import pallas as pl
from jax.experimental.pallas import tpu as pltpu
from jax.sharding import PartitionSpec as P

CHUNKS = 1
UNROLL = 8
MESH = pl.DeviceIdType.MESH
SEQUENCE = ("B1", "B2", "A1", "X1", "B3", "X2", "B4", "A2", "X3", "X4", "A3", "A4")


def kernel(
    x_in, i_in, l_in, r_in, o_ref, *scratch
):
    chunks = CHUNKS
    W = scratch[:chunks]
    (x_all, i_all, i_smem, part, acc, got_core, got_y,
     send_sem, swap_sem, h_sem, ax_sem, az_sem, bz_sem, bx_sem, x_sem, i_sem, red_sem, loc_sem) = scratch[chunks:]
    held, order = x_in.shape[0], x_in.shape[1]
    rows = order // chunks
    term, sector = lax.axis_index("term"), lax.axis_index("sector")
    p, z = term // 8, lax.rem(term, 8)
    h, x, c = sector // 8, lax.rem(sector // 2, 4), lax.rem(sector, 2)
    turn = 1 - 2 * c
    core = (term, sector + turn)
    across = (lax.rem(term + 8, 16), sector)
    twin = (term, lax.rem(sector + 8, 16))

    def z_at(k):
        return lax.rem(z + 16 + k * turn, 8)

    def x_at(k):
        return lax.rem(x + 8 + k * turn, 4)

    def z_dev(k):
        return (p * 8 + z_at(k), sector)

    def x_dev(k):
        return (term, h * 8 + x_at(k) * 2 + c)

    barrier = pltpu.get_barrier_semaphore()
    peers = (core, across, twin, z_dev(1), z_dev(-1), x_dev(1), x_dev(-1))
    for peer in peers:
        pl.semaphore_signal(barrier, inc=1, device_id=peer, device_id_type=MESH)
    pl.semaphore_wait(barrier, len(peers))

    pending = []

    def copy_of(src, dst, recv, device, number=0):
        return pltpu.make_async_remote_copy(
            src_ref=src, dst_ref=dst, send_sem=send_sem.at[number], recv_sem=recv,
            device_id=device, device_id_type=MESH,
        )

    def send(src, dst, recv, device):
        made = copy_of(src, dst, recv, device, len(pending))
        made.start()
        pending.append(made)

    def arrived(dst, recv):
        copy_of(dst, dst, recv, core).wait_recv()

    def width(q):
        return 2 + (chunks if q == 0 else 0)

    def b_at(q, xx):
        return 8 + xx * width(q)

    def item(q, e):
        return z_at(-e) if e <= 4 else z_at(e - 4)

    def a_pair(q, e, xx):
        return W[q].at[item(q, e), pl.ds(2 * xx, 2)]

    def a_row(q, e):
        return W[q].at[item(q, e), pl.ds(0, 8)]

    def b_item(q, e, xx):
        return W[q].at[item(q, e), pl.ds(b_at(q, xx), width(q))]

    local = []
    for q in range(chunks):
        mine = jnp.where(c == 0, 2 * x + h, b_at(q, x) + h)
        send(l_in.at[1 - c, q], W[q].at[z, mine], swap_sem.at[q], core)
        local.append(pltpu.make_async_copy(l_in.at[c, q], W[q].at[z, mine], loc_sem.at[q]))
        local[-1].start()
    right_own = pltpu.make_async_copy(
        r_in.at[c, x], W[0].at[z, pl.ds(b_at(0, x) + 2, chunks)], loc_sem.at[chunks])
    right_own.start()
    for q in range(chunks):
        other = jnp.where(c == 0, b_at(q, x) + h, 2 * x + h)
        local[q].wait()
        arrived(W[q].at[z, other], swap_sem.at[q])
        for kind, slot in ((0, 2 * x + h), (1, b_at(q, x) + h)):
            send(W[q].at[z, slot], W[q].at[z, slot], h_sem.at[q, kind], twin)
    right_own.wait()
    send(i_in, i_all.at[1], i_sem.at[1], core)
    send(i_in, i_all.at[2], i_sem.at[2], across)
    send(x_in, x_all.at[1], x_sem.at[1], core)
    send(x_in, x_all.at[2], x_sem.at[2], across)
    keep = pltpu.make_async_copy(i_in, i_all.at[0], loc_sem.at[chunks + 1])
    keep.start()
    keep_x = pltpu.make_async_copy(x_in, x_all.at[0], loc_sem.at[chunks + 2])
    keep_x.start()

    def x_sends(q, e):
        mine = b_item(q, e, x)
        send(mine, mine, bx_sem.at[q, e, 0], x_dev(1))
        send(mine, mine, bx_sem.at[q, e, 1], x_dev(-1))

    def x_forward(q, e):
        passed = b_item(q, e, x_at(-1))
        arrived(passed, bx_sem.at[q, e, 0])
        send(passed, passed, bx_sem.at[q, e, 2], x_dev(1))

    def opening(q):
        for kind, slot in ((0, 2 * x + 1 - h), (1, b_at(q, x) + 1 - h)):
            arrived(W[q].at[z, slot], h_sem.at[q, kind])
        mine = b_item(q, 0, x)
        send(mine, mine, bz_sem.at[q, 1], z_dev(1))
        send(mine, mine, bz_sem.at[q, 5], z_dev(-1))
        pair = a_pair(q, 0, x)
        send(pair, pair, ax_sem.at[q, 0], x_dev(1))
        send(pair, pair, ax_sem.at[q, 1], x_dev(-1))
        x_sends(q, 0)

    def row_ready(q):
        passed = a_pair(q, 0, x_at(-1))
        arrived(passed, ax_sem.at[q, 0])
        send(passed, passed, ax_sem.at[q, 2], x_dev(1))
        arrived(a_pair(q, 0, x_at(1)), ax_sem.at[q, 1])
        arrived(a_pair(q, 0, x_at(2)), ax_sem.at[q, 2])
        row = a_row(q, 0)
        send(row, row, az_sem.at[q, 1], z_dev(1))
        send(row, row, az_sem.at[q, 5], z_dev(-1))

    def tick(q, what, d):
        for e, last, way in ((d, 4, 1), (4 + d, 7, -1)):
            if e > last:
                continue
            if what == "A":
                row = a_row(q, e)
                arrived(row, az_sem.at[q, e])
                if e < last:
                    send(row, row, az_sem.at[q, e + 1], z_dev(way))
            if what == "B":
                mine = b_item(q, e, x)
                arrived(mine, bz_sem.at[q, e])
                if e < last:
                    send(mine, mine, bz_sem.at[q, e + 1], z_dev(way))
                x_sends(q, e)
            if what == "X":
                x_forward(q, e)

    def closing(q):
        for e in range(8):
            arrived(b_item(q, e, x_at(1)), bx_sem.at[q, e, 1])
            arrived(b_item(q, e, x_at(2)), bx_sem.at[q, e, 2])

    def others():
        arrived(i_all.at[1], i_sem.at[1])
        arrived(i_all.at[2], i_sem.at[2])
        send(i_all.at[2], i_all.at[3], i_sem.at[3], core)
        arrived(x_all.at[2], x_sem.at[2])
        send(x_all.at[2], x_all.at[3], x_sem.at[3], core)
        arrived(x_all.at[1], x_sem.at[1])
        keep.wait()
        keep_x.wait()
        arrived(i_all.at[3], i_sem.at[3])
        table = pltpu.make_async_copy(i_all, i_smem, loc_sem.at[chunks + 3])
        table.start()
        arrived(x_all.at[3], x_sem.at[3])
        table.wait()

    def products(q, group, store):
        def some(i, carry):
            for u in range(UNROLL):
                k = i * UNROLL + u
                left, right = i_smem[group, 0, k], i_smem[group, 0, held + k]
                spot, half, odd = (left >> 1) & 3, left >> 3, left & 1
                slot = jnp.where(odd == 0, 2 * spot + half, b_at(q, spot) + half)
                tall = jnp.concatenate([W[q][e, slot] for e in range(8)], axis=0)
                mixed = jnp.dot(
                    tall, x_all[group, k], preferred_element_type=jnp.float32
                ).astype(jnp.bfloat16)
                wide = jnp.concatenate(
                    [mixed[e * rows:(e + 1) * rows] for e in range(8)], axis=1)
                at = b_at(0, right) + 2
                chosen = jnp.concatenate(
                    [jnp.concatenate([W[0][e, at + i] for i in range(chunks)], axis=0)
                     for e in range(8)], axis=1)
                store(k, lax.dot_general(
                    wide, chosen, (((1,), (1,)), ((), ())),
                    preferred_element_type=jnp.float32))
            return carry
        lax.fori_loop(0, held // UNROLL, some, 0)

    def put(ref):
        def store(k, value):
            ref[k] = value.astype(ref.dtype)
        return store

    def reduce_steps(q):
        def first():
            products(q, 3, put(part.at[q, 0]))
            send(part.at[q, 0], got_core.at[q, 0], red_sem.at[q, 0], core)

        def second():
            products(q, 2, put(acc))
            arrived(got_core.at[q, 0], red_sem.at[q, 0])

            def join(k, carry):
                part[q, 1, k] = (acc[k] + got_core[q, 0, k].astype(jnp.float32)).astype(jnp.bfloat16)
                return carry
            lax.fori_loop(0, held, join, 0)
            send(part.at[q, 1], got_y.at[q], red_sem.at[q, 1], across)

        def third():
            products(q, 1, put(part.at[q, 2]))
            send(part.at[q, 2], got_core.at[q, 1], red_sem.at[q, 2], core)

        def fourth():
            products(q, 0, put(acc))
            arrived(got_core.at[q, 1], red_sem.at[q, 2])
            arrived(got_y.at[q], red_sem.at[q, 1])

            def join(k, carry):
                total = acc[k] + got_core[q, 1, k].astype(jnp.float32) + got_y[q, k].astype(jnp.float32)
                o_ref[k, pl.ds(q * rows, rows)] = total.astype(jnp.bfloat16)
                return carry
            lax.fori_loop(0, held, join, 0)
        return [first, second, third, fourth]

    for q in range(chunks):
        opening(q)
    for q in range(chunks):
        x_forward(q, 0)
        row_ready(q)
    waiting = []
    for q in range(chunks):
        steps = [functools.partial(tick, q, name[0], int(name[1])) for name in SEQUENCE]
        for number, step in enumerate(steps):
            step()
            if waiting and number % 3 == 2:
                waiting.pop(0)()
        closing(q)
        if q == 0:
            others()
        for step in waiting:
            step()
        waiting = reduce_steps(q)
    for step in waiting:
        step()
    for made in pending:
        made.wait_send()


def local(wavefunction, left_sector, right_sector, left_blocks, right_blocks):
    held, order = wavefunction.shape[:2]
    rows = order // CHUNKS
    index = jnp.concatenate([left_sector[:, 0], right_sector])
    index = jnp.pad(index[None], ((0, 7), (0, 128 - 2 * held)))
    left = left_blocks.reshape(2, CHUNKS, rows, order)
    right = right_blocks.reshape(2, 4, CHUNKS, rows, order)
    bf16 = jnp.bfloat16
    dma = pltpu.SemaphoreType.DMA
    scratch = [
        pltpu.VMEM((8, 8 + 4 * (2 + (CHUNKS if q == 0 else 0)), rows, order), bf16)
        for q in range(CHUNKS)
    ]
    scratch += [
        pltpu.VMEM((4, held, order, order), bf16),
        pltpu.VMEM((4, 8, 128), jnp.int32),
        pltpu.SMEM((4, 8, 128), jnp.int32),
        pltpu.VMEM((CHUNKS, 3, held, rows, order), bf16),
        pltpu.VMEM((held, rows, order), jnp.float32),
        pltpu.VMEM((CHUNKS, 2, held, rows, order), bf16),
        pltpu.VMEM((CHUNKS, held, rows, order), bf16),
        dma((6 + 50 * CHUNKS,)),
        dma((CHUNKS,)),
        dma((CHUNKS, 2)),
        dma((CHUNKS, 3)),
        dma((CHUNKS, 8)),
        dma((CHUNKS, 8)),
        dma((CHUNKS, 8, 3)),
        dma((4,)),
        dma((4,)),
        dma((CHUNKS, 3)),
        dma((CHUNKS + 4,)),
    ]
    vmem = pl.BlockSpec(memory_space=pltpu.VMEM)
    return pl.pallas_call(
        kernel,
        out_shape=jax.ShapeDtypeStruct(wavefunction.shape, wavefunction.dtype),
        in_specs=[vmem] * 4,
        out_specs=vmem,
        scratch_shapes=scratch,
        compiler_params=pltpu.CompilerParams(
            collective_id=0, has_side_effects=True, vmem_limit_bytes=48 * 1024 * 1024),
        name="terms",
    )(wavefunction, index, left, right)


def solution(mesh):
    placed = (
        P(("term", "sector"), None, None),
        P(("term", "sector"), None),
        P(("term", "sector")),
        P("term", "sector", None, None),
        P("term", None, None, None),
    )
    return jax.shard_map(
        local,
        mesh=mesh,
        in_specs=placed,
        out_specs=P(("term", "sector"), None, None),
        check_vma=False,
    )
```

```python
import functools

import jax
import jax.numpy as jnp
from jax import lax
from jax.experimental import pallas as pl
from jax.experimental.pallas import tpu as pltpu
from jax.sharding import PartitionSpec as P

CHUNKS = 2
PIECE = 8
MESH = pl.DeviceIdType.MESH
ORDER = (
    "0R", "1R", "0r", "0B1", "0X0", "0A1", "1r", "0B2", "0X1", "0A2", "0B3", "0X2", "0A3",
    "0B4", "0X3", "0A4", "1B1", "1X0", "1A1", "0X4", "1B2", "1X1", "1A2", "0C", "O", "0P0",
    "0P1", "1B3", "1X2", "1A3", "0P2", "0P3", "1B4", "1X3", "1A4", "0P4", "0P5", "1X4", "0P6",
    "0P7", "1C", "1P0", "1P1", "1P2", "1P3", "1P4", "1P5", "1P6", "1P7",
)


def kernel(x_in, i_in, l_in, r_in, o_ref, *scratch):
    chunks = CHUNKS
    W = scratch[:chunks]
    (x_all, i_all, i_smem, r_own, part, acc, got_core, got_y,
     send_sem, head_sem, a_sem, b_sem, az_sem, bz_sem, bx_sem, x_sem, i_sem, red_sem,
     loc_sem) = scratch[chunks:]
    held, order = x_in.shape[0], x_in.shape[1]
    rows = order // chunks
    term, sector = lax.axis_index("term"), lax.axis_index("sector")
    p, z = term // 8, lax.rem(term, 8)
    h, x, c = sector // 8, lax.rem(sector // 2, 4), lax.rem(sector, 2)
    turn = 1 - 2 * c
    core = (term, sector + turn)
    across = (lax.rem(term + 8, 16), sector)

    def z_at(k):
        return lax.rem(z + 16 + k * turn, 8)

    def x_at(k):
        return lax.rem(x + 8 + k * turn, 4)

    def z_dev(k):
        return (p * 8 + z_at(k), sector)

    def x_dev(k):
        return (term, h * 8 + x_at(k) * 2 + c)

    def plane(dh, dx, core_index):
        return (term, lax.rem(h + dh, 2) * 8 + lax.rem(x + dx, 4) * 2 + core_index)

    def width(q):
        return 2 + (chunks if q == 0 else 0)

    def b_at(q, xx):
        return 8 + xx * width(q)

    def item(e):
        return z_at(-e) if e <= 4 else z_at(e - 4)

    def a_half(q, e, half):
        return W[q].at[item(e), pl.ds(4 * half, 4)]

    def b_item(q, e, xx):
        return W[q].at[item(e), pl.ds(b_at(q, xx), width(q))]

    right_own = pltpu.make_async_copy(r_in.at[c, x], r_own, loc_sem.at[0])
    right_own.start()
    keep = pltpu.make_async_copy(i_in, i_all.at[0], loc_sem.at[1])
    keep.start()
    keep_x = pltpu.make_async_copy(x_in, x_all.at[0], loc_sem.at[2])
    keep_x.start()

    barrier = pltpu.get_barrier_semaphore()
    peers = [across, z_dev(1), z_dev(-1), core]
    for dh in range(2):
        for dx in range(4):
            if dh or dx:
                peers += [plane(dh, dx, 0), plane(dh, dx, 1)]
    for peer in peers:
        pl.semaphore_signal(barrier, inc=1, device_id=peer, device_id_type=MESH)

    right_own.wait()
    turned = r_own[...].T
    for i in range(chunks):
        W[0][z, b_at(0, x) + 2 + i] = turned[i * rows:(i + 1) * rows]

    pl.semaphore_wait(barrier, len(peers))

    pending, head0, head1 = [], [], []

    def send(src, dst, recv, device, kept=None):
        kept, sems = (pending, send_sem) if kept is None else (kept, head_sem)
        made = pltpu.make_async_remote_copy(
            src_ref=src, dst_ref=dst, send_sem=sems.at[len(kept)], recv_sem=recv,
            device_id=device, device_id_type=MESH)
        made.start()
        kept.append(made)

    def arrived(dst, recv):
        pltpu.make_async_remote_copy(
            src_ref=dst, dst_ref=dst, send_sem=send_sem.at[0], recv_sem=recv,
            device_id=core, device_id_type=MESH).wait_recv()

    def own_copy(q):
        slot = jnp.where(c == 0, 2 * x + h, b_at(q, x) + h)
        return pltpu.make_async_copy(l_in.at[c, q], W[q].at[z, slot], loc_sem.at[3 + q])

    for q in range(chunks):
        own_copy(q).start()

        @pl.when(c == 1)
        def _():
            slot = b_at(q, x) + h
            send(l_in.at[0, q], W[q].at[z, slot], b_sem.at[q, 0], core, head1)
            for j in range(2):
                send(l_in.at[j, q], W[q].at[z, slot], b_sem.at[q, 1], plane(1, 0, j), head1)

        @pl.when(c == 0)
        def _():
            slot = 2 * x + h
            for dh, dx in ((1, 2), (0, 2), (1, 1), (1, 3), (1, 0), (0, 1), (0, 3)):
                for j in range(2):
                    send(l_in.at[j, q], W[q].at[z, slot], a_sem.at[q, dh * 4 + dx],
                         plane(dh, dx, j), head0)
            send(l_in.at[1, q], W[q].at[z, slot], a_sem.at[q, 0], core, head0)

    def x_sends(q, e):
        mine = b_item(q, e, x)
        send(mine, mine, bx_sem.at[q, e, 0], x_dev(1))
        send(mine, mine, bx_sem.at[q, e, 1], x_dev(-1))

    def column_ready(q):
        @pl.when(c == 0)
        def _():
            arrived(W[q].at[z, b_at(q, x) + h], b_sem.at[q, 0])

        @pl.when(c == 1)
        def _():
            own_copy(q).wait()
        arrived(W[q].at[z, b_at(q, x) + 1 - h], b_sem.at[q, 1])
        mine = b_item(q, 0, x)
        send(mine, mine, bz_sem.at[q, 1], z_dev(1))
        send(mine, mine, bz_sem.at[q, 5], z_dev(-1))
        x_sends(q, 0)

    def row_ready(q):
        @pl.when(c == 0)
        def _():
            own_copy(q).wait()

        @pl.when(c == 1)
        def _():
            arrived(W[q].at[z, 2 * x + h], a_sem.at[q, 0])
        for dh in range(2):
            for dx in range(4):
                if dh or dx:
                    slot = 2 * lax.rem(x + 4 - dx, 4) + lax.rem(h + dh, 2)
                    arrived(W[q].at[z, slot], a_sem.at[q, dh * 4 + dx])
        for half in range(2):
            row = a_half(q, 0, half)
            send(row, row, az_sem.at[q, 1, half], z_dev(1))
            send(row, row, az_sem.at[q, 5, half], z_dev(-1))

    def ways(d):
        return [w for w in ((d, 4, 1), (4 + d, 7, -1)) if w[0] <= w[1]]

    def tick_a(q, d):
        for half in range(2):
            for e, last, way in ways(d):
                row = a_half(q, e, half)
                arrived(row, az_sem.at[q, e, half])
                if e < last:
                    send(row, row, az_sem.at[q, e + 1, half], z_dev(way))

    def tick_b(q, d):
        for e, last, way in ways(d):
            mine = b_item(q, e, x)
            arrived(mine, bz_sem.at[q, e])
            if e < last:
                send(mine, mine, bz_sem.at[q, e + 1], z_dev(way))
            x_sends(q, e)

    def tick_x(q, d):
        for e in ((0,) if d == 0 else [w[0] for w in ways(d)]):
            passed = b_item(q, e, x_at(-1))
            arrived(passed, bx_sem.at[q, e, 0])
            send(passed, passed, bx_sem.at[q, e, 2], x_dev(1))

    def closing(q):
        for e in range(8):
            arrived(b_item(q, e, x_at(1)), bx_sem.at[q, e, 1])
            arrived(b_item(q, e, x_at(2)), bx_sem.at[q, e, 2])

    def exchange():
        send(i_in, i_all.at[1], i_sem.at[1], core)
        send(i_in, i_all.at[2], i_sem.at[2], across)
        send(x_in, x_all.at[1], x_sem.at[1], core)
        send(x_in, x_all.at[2], x_sem.at[2], across)

    def others():
        arrived(i_all.at[1], i_sem.at[1])
        arrived(i_all.at[2], i_sem.at[2])
        send(i_all.at[2], i_all.at[3], i_sem.at[3], core)
        arrived(x_all.at[2], x_sem.at[2])
        send(x_all.at[2], x_all.at[3], x_sem.at[3], core)
        arrived(x_all.at[1], x_sem.at[1])
        keep.wait()
        keep_x.wait()
        arrived(i_all.at[3], i_sem.at[3])
        table = pltpu.make_async_copy(i_all, i_smem, loc_sem.at[3 + chunks])
        table.start()
        arrived(x_all.at[3], x_sem.at[3])
        table.wait()

    def products(q, group, first, store):
        for u in range(PIECE):
            k = first + u
            left, right = i_smem[group, 0, k], i_smem[group, 0, held + k]
            spot, half, odd = (left >> 1) & 3, left >> 3, left & 1
            slot = jnp.where(odd == 0, 2 * spot + half, b_at(q, spot) + half)
            tall = jnp.concatenate([W[q][e, slot] for e in range(8)], axis=0)
            mixed = jnp.dot(
                tall, x_all[group, k], preferred_element_type=jnp.float32
            ).astype(jnp.bfloat16)
            wide = jnp.concatenate([mixed[e * rows:(e + 1) * rows] for e in range(8)], axis=1)
            at = b_at(0, right) + 2
            chosen = jnp.concatenate(
                [W[0][e, at + i] for e in range(8) for i in range(chunks)], axis=0)
            store(k, jnp.dot(wide, chosen, preferred_element_type=jnp.float32))

    def piece(q, number):
        stage, first = number // 2, (number % 2) * PIECE
        span = pl.ds(first, PIECE)

        def to_part(k, value):
            part[q, stage, k] = value.astype(jnp.bfloat16)

        def to_acc(k, value):
            acc[k] = value
        if stage == 0:
            products(q, 3, first, to_part)
            send(part.at[q, 0, span], got_core.at[q, 0, span], red_sem.at[q, 0, number % 2], core)
        if stage == 1:
            products(q, 2, first, to_acc)
            arrived(got_core.at[q, 0, span], red_sem.at[q, 0, number % 2])
            part[q, 1, span] = (
                acc[span] + got_core[q, 0, span].astype(jnp.float32)).astype(jnp.bfloat16)
            send(part.at[q, 1, span], got_y.at[q, span], red_sem.at[q, 1, number % 2], across)
        if stage == 2:
            products(q, 1, first, to_part)
            send(part.at[q, 2, span], got_core.at[q, 1, span], red_sem.at[q, 2, number % 2], core)
        if stage == 3:
            products(q, 0, first, to_acc)
            arrived(got_core.at[q, 1, span], red_sem.at[q, 2, number % 2])
            arrived(got_y.at[q, span], red_sem.at[q, 1, number % 2])
            total = (acc[span] + got_core[q, 1, span].astype(jnp.float32)
                     + got_y[q, span].astype(jnp.float32))
            o_ref[span, pl.ds(q * rows, rows)] = total.astype(jnp.bfloat16)

    for name in ORDER:
        if name == "O":
            others()
            continue
        q, what, d = int(name[0]), name[1], int(name[2:] or 0)
        if what == "R":
            column_ready(q)
        if what == "r":
            row_ready(q)
            if q == 0:
                exchange()
        if what == "A":
            tick_a(q, d)
        if what == "B":
            tick_b(q, d)
        if what == "X":
            tick_x(q, d)
        if what == "C":
            closing(q)
        if what == "P":
            piece(q, d)

    for made in pending:
        made.wait_send()
    for kept, index in ((head0, 0), (head1, 1)):
        @pl.when(c == index)
        def _():
            for number in range(len(kept)):
                pltpu.make_async_remote_copy(
                    src_ref=l_in.at[0, 0], dst_ref=W[0].at[0, 0], send_sem=head_sem.at[number],
                    recv_sem=a_sem.at[0, 0], device_id=core, device_id_type=MESH).wait_send()


def local(wavefunction, left_sector, right_sector, left_blocks, right_blocks):
    held, order = wavefunction.shape[:2]
    rows = order // CHUNKS
    index = jnp.concatenate([left_sector[:, 0], right_sector])
    index = jnp.pad(index[None], ((0, 7), (0, 128 - 2 * held)))
    left = left_blocks.reshape(2, CHUNKS, rows, order)
    bf16 = jnp.bfloat16
    dma = pltpu.SemaphoreType.DMA
    scratch = [
        pltpu.VMEM((8, 8 + 4 * (2 + (CHUNKS if q == 0 else 0)), rows, order), bf16)
        for q in range(CHUNKS)
    ]
    scratch += [
        pltpu.VMEM((4, held, order, order), bf16),
        pltpu.VMEM((4, 8, 128), jnp.int32),
        pltpu.SMEM((4, 8, 128), jnp.int32),
        pltpu.VMEM((order, order), bf16),
        pltpu.VMEM((CHUNKS, 3, held, rows, order), bf16),
        pltpu.VMEM((held, rows, order), jnp.float32),
        pltpu.VMEM((CHUNKS, 2, held, rows, order), bf16),
        pltpu.VMEM((CHUNKS, held, rows, order), bf16),
        dma((6 + 60 * CHUNKS,)),
        dma((15 * CHUNKS,)),
        dma((CHUNKS, 8)),
        dma((CHUNKS, 2)),
        dma((CHUNKS, 8, 2)),
        dma((CHUNKS, 8)),
        dma((CHUNKS, 8, 3)),
        dma((4,)),
        dma((4,)),
        dma((CHUNKS, 3, 2)),
        dma((CHUNKS + 4,)),
    ]
    vmem, anywhere = pl.BlockSpec(memory_space=pltpu.VMEM), pl.BlockSpec(memory_space=pl.ANY)
    return pl.pallas_call(
        kernel,
        out_shape=jax.ShapeDtypeStruct(wavefunction.shape, wavefunction.dtype),
        in_specs=[anywhere, vmem, anywhere, anywhere],
        out_specs=vmem,
        scratch_shapes=scratch,
        compiler_params=pltpu.CompilerParams(
            collective_id=0, has_side_effects=True, vmem_limit_bytes=56 * 1024 * 1024),
        name="terms",
    )(wavefunction, index, left, right_blocks)


def solution(mesh):
    placed = (
        P(("term", "sector"), None, None),
        P(("term", "sector"), None),
        P(("term", "sector")),
        P("term", "sector", None, None),
        P("term", None, None, None),
    )
    return jax.shard_map(
        local,
        mesh=mesh,
        in_specs=placed,
        out_specs=P(("term", "sector"), None, None),
        check_vma=False,
    )
```

```python
import functools

import jax
import jax.numpy as jnp
from jax import lax
from jax.experimental import pallas as pl
from jax.experimental.pallas import tpu as pltpu
from jax.sharding import PartitionSpec as P

CHUNKS = 2
PIECE = 8
MESH = pl.DeviceIdType.MESH
ORDER = (
    "0R", "1R", "0r", "0B1", "0X0", "0A1", "1r", "0B2", "0X1", "0A2", "0B3", "0X2", "0A3",
    "0B4", "0X3", "0A4", "1B1", "1X0", "1A1", "0X4", "1B2", "1X1", "1A2", "0C", "O", "0P0",
    "0P1", "1B3", "1X2", "1A3", "0P2", "0P3", "1B4", "1X3", "1A4", "0P4", "0P5", "1X4", "0P6",
    "0P7", "1C", "1P0", "1P1", "1P2", "1P3", "1P4", "1P5", "1P6", "1P7",
)


def kernel(x_in, i_in, l_in, r_in, o_ref, *scratch):
    chunks = CHUNKS
    W = scratch[:chunks]
    (x_all, i_all, i_smem, r_own, part, acc, got_core, got_y,
     send_sem, head_sem, a_sem, b_sem, az_sem, bz_sem, bx_sem, x_sem, i_sem, red_sem,
     loc_sem) = scratch[chunks:]
    held, order = x_in.shape[0], x_in.shape[1]
    rows = order // chunks
    term, sector = lax.axis_index("term"), lax.axis_index("sector")
    p, z = term // 8, lax.rem(term, 8)
    h, x, c = sector // 8, lax.rem(sector // 2, 4), lax.rem(sector, 2)
    turn = 1 - 2 * c
    core = (term, sector + turn)
    across = ((lax.rem(term + 8, 16), sector),
              (lax.rem(term + 8, 16), lax.rem(sector + 8, 16)))

    def z_at(k):
        return lax.rem(z + 16 + k * turn, 8)

    def x_at(k):
        return lax.rem(x + 8 + k * turn, 4)

    def z_dev(k):
        return (p * 8 + z_at(k), sector)

    def x_dev(k):
        return (term, h * 8 + x_at(k) * 2 + c)

    def plane(dh, dx, core_index):
        return (term, lax.rem(h + dh, 2) * 8 + lax.rem(x + dx, 4) * 2 + core_index)

    def width(q):
        return 2 + (chunks if q == 0 else 0)

    def b_at(q, xx):
        return 8 + xx * width(q)

    def a_half(q, e, half):
        return W[q].at[e, pl.ds(4 * half, 4)]

    def b_item(q, e, xx):
        return W[q].at[e, pl.ds(b_at(q, xx), width(q))]

    right_own = pltpu.make_async_copy(r_in.at[c, x], r_own, loc_sem.at[0])
    right_own.start()
    keep = pltpu.make_async_copy(i_in, i_all.at[0], loc_sem.at[1])
    keep.start()
    keep_x = pltpu.make_async_copy(x_in, x_all.at[0], loc_sem.at[2])
    keep_x.start()

    barrier = pltpu.get_barrier_semaphore()
    peers = [*across, z_dev(1), z_dev(-1), core]
    for dh in range(2):
        for dx in range(4):
            if dh or dx:
                peers += [plane(dh, dx, 0), plane(dh, dx, 1)]
    for peer in peers:
        pl.semaphore_signal(barrier, inc=1, device_id=peer, device_id_type=MESH)

    right_own.wait()
    turned = r_own[...].T
    for i in range(chunks):
        W[0][0, b_at(0, x) + 2 + i] = turned[i * rows:(i + 1) * rows]

    pl.semaphore_wait(barrier, len(peers))

    pending, head0, head1 = [], [], []

    def send(src, dst, recv, device, kept=None):
        kept, sems = (pending, send_sem) if kept is None else (kept, head_sem)
        made = pltpu.make_async_remote_copy(
            src_ref=src, dst_ref=dst, send_sem=sems.at[len(kept)], recv_sem=recv,
            device_id=device, device_id_type=MESH)
        made.start()
        kept.append(made)

    def arrived(dst, recv):
        pltpu.make_async_remote_copy(
            src_ref=dst, dst_ref=dst, send_sem=send_sem.at[0], recv_sem=recv,
            device_id=core, device_id_type=MESH).wait_recv()

    def own_copy(q):
        slot = jnp.where(c == 0, 2 * x + h, b_at(q, x) + h)
        return pltpu.make_async_copy(l_in.at[c, q], W[q].at[0, slot], loc_sem.at[3 + q])

    for q in range(chunks):
        own_copy(q).start()

        @pl.when(c == 1)
        def _():
            slot = b_at(q, x) + h
            send(l_in.at[0, q], W[q].at[0, slot], b_sem.at[q, 0], core, head1)
            for j in range(2):
                send(l_in.at[j, q], W[q].at[0, slot], b_sem.at[q, 1], plane(1, 0, j), head1)

        @pl.when(c == 0)
        def _():
            slot = 2 * x + h
            for dh, dx in ((1, 2), (0, 2), (1, 1), (1, 3), (1, 0), (0, 1), (0, 3)):
                for j in range(2):
                    send(l_in.at[j, q], W[q].at[0, slot], a_sem.at[q, dh * 4 + dx],
                         plane(dh, dx, j), head0)
            send(l_in.at[1, q], W[q].at[0, slot], a_sem.at[q, 0], core, head0)

    def x_sends(q, e):
        mine = b_item(q, e, x)
        send(mine, mine, bx_sem.at[q, e, 0], x_dev(1))
        send(mine, mine, bx_sem.at[q, e, 1], x_dev(-1))

    def column_ready(q):
        @pl.when(c == 0)
        def _():
            arrived(W[q].at[0, b_at(q, x) + h], b_sem.at[q, 0])

        @pl.when(c == 1)
        def _():
            own_copy(q).wait()
        arrived(W[q].at[0, b_at(q, x) + 1 - h], b_sem.at[q, 1])
        mine = b_item(q, 0, x)
        send(mine, b_item(q, 1, x), bz_sem.at[q, 1], z_dev(1))
        send(mine, b_item(q, 5, x), bz_sem.at[q, 5], z_dev(-1))
        x_sends(q, 0)

    def row_ready(q):
        @pl.when(c == 0)
        def _():
            own_copy(q).wait()

        @pl.when(c == 1)
        def _():
            arrived(W[q].at[0, 2 * x + h], a_sem.at[q, 0])
        for dh in range(2):
            for dx in range(4):
                if dh or dx:
                    slot = 2 * lax.rem(x + 4 - dx, 4) + lax.rem(h + dh, 2)
                    arrived(W[q].at[0, slot], a_sem.at[q, dh * 4 + dx])
        for half in range(2):
            row = a_half(q, 0, half)
            send(row, a_half(q, 1, half), az_sem.at[q, 1, half], z_dev(1))
            send(row, a_half(q, 5, half), az_sem.at[q, 5, half], z_dev(-1))

    def ways(d):
        return [w for w in ((d, 4, 1), (4 + d, 7, -1)) if w[0] <= w[1]]

    def tick_a(q, d):
        for half in range(2):
            for e, last, way in ways(d):
                row = a_half(q, e, half)
                arrived(row, az_sem.at[q, e, half])
                if e < last:
                    send(row, a_half(q, e + 1, half), az_sem.at[q, e + 1, half], z_dev(way))

    def tick_b(q, d):
        for e, last, way in ways(d):
            mine = b_item(q, e, x)
            arrived(mine, bz_sem.at[q, e])
            if e < last:
                send(mine, b_item(q, e + 1, x), bz_sem.at[q, e + 1], z_dev(way))
            x_sends(q, e)

    def tick_x(q, d):
        for e in ((0,) if d == 0 else [w[0] for w in ways(d)]):
            passed = b_item(q, e, x_at(-1))
            arrived(passed, bx_sem.at[q, e, 0])
            send(passed, passed, bx_sem.at[q, e, 2], x_dev(1))

    def closing(q):
        for e in range(8):
            arrived(b_item(q, e, x_at(1)), bx_sem.at[q, e, 1])
            arrived(b_item(q, e, x_at(2)), bx_sem.at[q, e, 2])

    def exchange():
        send(i_in, i_all.at[1], i_sem.at[1], core)
        send(x_in, x_all.at[1], x_sem.at[1], core)
        for side in range(2):
            span = pl.ds(side * PIECE, PIECE)
            send(i_in, i_all.at[2 + 2 * side], i_sem.at[2 + 2 * side], across[side])
            send(x_in.at[span], x_all.at[2, span], x_sem.at[2 + 2 * side], across[side])

    def others():
        arrived(i_all.at[1], i_sem.at[1])
        for side in range(2):
            span = pl.ds(side * PIECE, PIECE)
            got, passed = 2 + 2 * side, 3 + 2 * side
            arrived(i_all.at[got], i_sem.at[got])
            send(i_all.at[got], i_all.at[passed], i_sem.at[passed], core)
            arrived(x_all.at[2, span], x_sem.at[got])
            send(x_all.at[2, span], x_all.at[3, span], x_sem.at[passed], core)
        arrived(x_all.at[1], x_sem.at[1])
        keep.wait()
        keep_x.wait()
        arrived(i_all.at[3], i_sem.at[3])
        arrived(i_all.at[5], i_sem.at[5])
        table = pltpu.make_async_copy(i_all, i_smem, loc_sem.at[3 + chunks])
        table.start()
        for side in range(2):
            span = pl.ds(side * PIECE, PIECE)
            arrived(x_all.at[3, span], x_sem.at[3 + 2 * side])
        table.wait()

    def products(q, group, first, store):
        terms = range(8)
        many = len(terms)
        halves = []
        for k in range(first, first + PIECE):
            table = group + 2 if group >= 2 and k >= PIECE else group
            left = i_smem[table, 0, k]
            spot, half, odd = (left >> 1) & 3, left >> 3, left & 1
            slot = jnp.where(odd == 0, 2 * spot + half, b_at(q, spot) + half)
            tall = jnp.concatenate([W[q][e, slot] for e in terms], axis=0)
            halves.append(jnp.dot(
                tall, x_all[group, k], preferred_element_type=jnp.float32
            ).astype(jnp.bfloat16))
        for k, mixed in zip(range(first, first + PIECE), halves):
            table = group + 2 if group >= 2 and k >= PIECE else group
            wide = jnp.concatenate([mixed[e * rows:(e + 1) * rows] for e in range(many)], axis=1)
            at = b_at(0, i_smem[table, 0, held + k]) + 2
            chosen = jnp.concatenate(
                [W[0][e, at + i] for e in terms for i in range(chunks)], axis=0)
            store(k, jnp.dot(wide, chosen, preferred_element_type=jnp.float32))

    def piece(q, number):
        stage, first = number // 2, (number % 2) * PIECE
        span = pl.ds(first, PIECE)

        def to_part(k, value):
            part[q, stage, k] = value.astype(jnp.bfloat16)

        def to_acc(k, value):
            acc[k] = value
        if stage == 0:
            products(q, 3, first, to_part)
            send(part.at[q, 0, span], got_core.at[q, 0, span], red_sem.at[q, 0, number % 2], core)
        if stage == 1:
            products(q, 2, first, to_acc)
            arrived(got_core.at[q, 0, span], red_sem.at[q, 0, number % 2])
            part[q, 1, span] = (
                acc[span] + got_core[q, 0, span].astype(jnp.float32)).astype(jnp.bfloat16)
            send(part.at[q, 1, span], got_y.at[q, span], red_sem.at[q, 1, number % 2],
                 across[number % 2])
        if stage == 2:
            products(q, 1, first, to_part)
            send(part.at[q, 2, span], got_core.at[q, 1, span], red_sem.at[q, 2, number % 2], core)
        if stage == 3:
            products(q, 0, first, to_acc)
            arrived(got_core.at[q, 1, span], red_sem.at[q, 2, number % 2])
            arrived(got_y.at[q, span], red_sem.at[q, 1, number % 2])
            total = (acc[span] + got_core[q, 1, span].astype(jnp.float32)
                     + got_y[q, span].astype(jnp.float32))
            o_ref[span, pl.ds(q * rows, rows)] = total.astype(jnp.bfloat16)

    for name in ORDER:
        if name == "O":
            others()
            continue
        q, what, d = int(name[0]), name[1], int(name[2:] or 0)
        if what == "R":
            column_ready(q)
        if what == "r":
            row_ready(q)
            if q == 0:
                exchange()
        if what == "A":
            tick_a(q, d)
        if what == "B":
            tick_b(q, d)
        if what == "X":
            tick_x(q, d)
        if what == "C":
            closing(q)
        if what == "P":
            piece(q, d)

    for made in pending:
        made.wait_send()
    for kept, index in ((head0, 0), (head1, 1)):
        @pl.when(c == index)
        def _():
            for number in range(len(kept)):
                pltpu.make_async_remote_copy(
                    src_ref=l_in.at[0, 0], dst_ref=W[0].at[0, 0], send_sem=head_sem.at[number],
                    recv_sem=a_sem.at[0, 0], device_id=core, device_id_type=MESH).wait_send()


def local(wavefunction, left_sector, right_sector, left_blocks, right_blocks):
    held, order = wavefunction.shape[:2]
    rows = order // CHUNKS
    index = jnp.concatenate([left_sector[:, 0], right_sector])
    index = jnp.pad(index[None], ((0, 7), (0, 128 - 2 * held)))
    left = left_blocks.reshape(2, CHUNKS, rows, order)
    bf16 = jnp.bfloat16
    dma = pltpu.SemaphoreType.DMA
    scratch = [
        pltpu.VMEM((8, 8 + 4 * (2 + (CHUNKS if q == 0 else 0)), rows, order), bf16)
        for q in range(CHUNKS)
    ]
    scratch += [
        pltpu.VMEM((4, held, order, order), bf16),
        pltpu.VMEM((6, 8, 128), jnp.int32),
        pltpu.SMEM((6, 8, 128), jnp.int32),
        pltpu.VMEM((order, order), bf16),
        pltpu.VMEM((CHUNKS, 3, held, rows, order), bf16),
        pltpu.VMEM((held, rows, order), jnp.float32),
        pltpu.VMEM((CHUNKS, 2, held, rows, order), bf16),
        pltpu.VMEM((CHUNKS, held, rows, order), bf16),
        dma((12 + 60 * CHUNKS,)),
        dma((15 * CHUNKS,)),
        dma((CHUNKS, 8)),
        dma((CHUNKS, 2)),
        dma((CHUNKS, 8, 2)),
        dma((CHUNKS, 8)),
        dma((CHUNKS, 8, 3)),
        dma((6,)),
        dma((6,)),
        dma((CHUNKS, 3, 2)),
        dma((CHUNKS + 4,)),
    ]
    vmem, anywhere = pl.BlockSpec(memory_space=pltpu.VMEM), pl.BlockSpec(memory_space=pl.ANY)
    return pl.pallas_call(
        kernel,
        out_shape=jax.ShapeDtypeStruct(wavefunction.shape, wavefunction.dtype),
        in_specs=[anywhere, vmem, anywhere, anywhere],
        out_specs=vmem,
        scratch_shapes=scratch,
        compiler_params=pltpu.CompilerParams(
            collective_id=0, has_side_effects=True, vmem_limit_bytes=56 * 1024 * 1024),
        name="terms",
    )(wavefunction, index, left, right_blocks)


def solution(mesh):
    placed = (
        P(("term", "sector"), None, None),
        P(("term", "sector"), None),
        P(("term", "sector")),
        P("term", "sector", None, None),
        P("term", None, None, None),
    )
    return jax.shard_map(
        local,
        mesh=mesh,
        in_specs=placed,
        out_specs=P(("term", "sector"), None, None),
        check_vma=False,
    )
```

```python
import functools

import jax
import jax.numpy as jnp
from jax import lax
from jax.experimental import pallas as pl
from jax.experimental.pallas import tpu as pltpu
from jax.sharding import PartitionSpec as P

CHUNKS = 2
PIECE = 8
MESH = pl.DeviceIdType.MESH
ORDER = (
    "0R", "1R", "0r", "0B1", "0X0", "0A1", "0B2", "0X1", "0A2", "1r", "0B3", "0X2", "0A3", "o",
    "0B4", "0X3", "1B1", "1X0", "1A1", "0X4", "1B2", "1X1", "1A2", "0A4", "0K0", "0K1", "0K2",
    "0K3", "0K4", "O", "0P0", "1B3", "1X2", "1A3", "0P1", "0P2", "1B4", "0P3", "1X3", "0P4",
    "1X4", "0P5", "0P6", "0P7", "1A4", "1K0", "1K1", "1K2", "1K3", "1K4", "1P0", "1P1", "1P2",
    "1P3", "1P4", "1P5", "1P6", "1P7",
)


def kernel(x_in, i_in, l_in, r_in, o_ref, *scratch):
    chunks = CHUNKS
    W = scratch[:chunks]
    (x_all, i_all, i_smem, r_own, part, acc, got_core, got_y,
     send_sem, head_sem, a_sem, b_sem, az_sem, bz_sem, bx_sem, x_sem, i_sem, red_sem,
     loc_sem) = scratch[chunks:]
    held, order = x_in.shape[0], x_in.shape[1]
    rows = order // chunks
    term, sector = lax.axis_index("term"), lax.axis_index("sector")
    p, z = term // 8, lax.rem(term, 8)
    h, x, c = sector // 8, lax.rem(sector // 2, 4), lax.rem(sector, 2)
    turn = 1 - 2 * c
    core = (term, sector + turn)
    across = ((lax.rem(term + 8, 16), sector),
              (lax.rem(term + 8, 16), lax.rem(sector + 8, 16)))

    def z_at(k):
        return lax.rem(z + 16 + k * turn, 8)

    def x_at(k):
        return lax.rem(x + 8 + k * turn, 4)

    def z_dev(k):
        return (p * 8 + z_at(k), sector)

    def x_dev(k):
        return (term, h * 8 + x_at(k) * 2 + c)

    def plane(dh, dx, core_index):
        return (term, lax.rem(h + dh, 2) * 8 + lax.rem(x + dx, 4) * 2 + core_index)

    def width(q):
        return 2 + (chunks if q == 0 else 0)

    def b_at(q, xx):
        return 8 + xx * width(q)

    def a_half(q, e, half):
        return W[q].at[e, pl.ds(4 * half, 4)]

    def b_item(q, e, xx):
        return W[q].at[e, pl.ds(b_at(q, xx), width(q))]

    right_own = pltpu.make_async_copy(r_in.at[c, x], r_own, loc_sem.at[0])
    right_own.start()
    keep = pltpu.make_async_copy(i_in, i_all.at[0], loc_sem.at[1])
    keep.start()
    keep_x = pltpu.make_async_copy(x_in, x_all.at[0], loc_sem.at[2])
    keep_x.start()

    barrier = pltpu.get_barrier_semaphore()
    peers = [*across, z_dev(1), z_dev(-1), core]
    for dh in range(2):
        for dx in range(4):
            if dh or dx:
                peers += [plane(dh, dx, 0), plane(dh, dx, 1)]
    for peer in peers:
        pl.semaphore_signal(barrier, inc=1, device_id=peer, device_id_type=MESH)

    right_own.wait()
    turned = r_own[...].T
    for i in range(chunks):
        W[0][0, b_at(0, x) + 2 + i] = turned[i * rows:(i + 1) * rows]

    pl.semaphore_wait(barrier, len(peers))

    pending, head0, head1 = [], [], []

    def send(src, dst, recv, device, kept=None):
        kept, sems = (pending, send_sem) if kept is None else (kept, head_sem)
        made = pltpu.make_async_remote_copy(
            src_ref=src, dst_ref=dst, send_sem=sems.at[len(kept)], recv_sem=recv,
            device_id=device, device_id_type=MESH)
        made.start()
        kept.append(made)

    def arrived(dst, recv):
        pltpu.make_async_remote_copy(
            src_ref=dst, dst_ref=dst, send_sem=send_sem.at[0], recv_sem=recv,
            device_id=core, device_id_type=MESH).wait_recv()

    def own_copy(q):
        slot = jnp.where(c == 0, 2 * x + h, b_at(q, x) + h)
        return pltpu.make_async_copy(l_in.at[c, q], W[q].at[0, slot], loc_sem.at[3 + q])

    for q in range(chunks):
        own_copy(q).start()

        @pl.when(c == 1)
        def _():
            slot = b_at(q, x) + h
            send(l_in.at[0, q], W[q].at[0, slot], b_sem.at[q, 0], core, head1)
            for j in range(2):
                send(l_in.at[j, q], W[q].at[0, slot], b_sem.at[q, 1], plane(1, 0, j), head1)

        @pl.when(c == 0)
        def _():
            slot = 2 * x + h
            for dh, dx in ((1, 2), (0, 2), (1, 1), (1, 3), (1, 0), (0, 1), (0, 3)):
                for j in range(2):
                    send(l_in.at[j, q], W[q].at[0, slot], a_sem.at[q, dh * 4 + dx],
                         plane(dh, dx, j), head0)
            send(l_in.at[1, q], W[q].at[0, slot], a_sem.at[q, 0], core, head0)

    def x_sends(q, e):
        mine = b_item(q, e, x)
        send(mine, mine, bx_sem.at[q, e, 0], x_dev(1))
        send(mine, mine, bx_sem.at[q, e, 1], x_dev(-1))

    def column_ready(q):
        @pl.when(c == 0)
        def _():
            arrived(W[q].at[0, b_at(q, x) + h], b_sem.at[q, 0])

        @pl.when(c == 1)
        def _():
            own_copy(q).wait()
        arrived(W[q].at[0, b_at(q, x) + 1 - h], b_sem.at[q, 1])
        mine = b_item(q, 0, x)
        send(mine, b_item(q, 1, x), bz_sem.at[q, 1], z_dev(1))
        send(mine, b_item(q, 5, x), bz_sem.at[q, 5], z_dev(-1))
        x_sends(q, 0)

    def row_ready(q):
        @pl.when(c == 0)
        def _():
            own_copy(q).wait()

        @pl.when(c == 1)
        def _():
            arrived(W[q].at[0, 2 * x + h], a_sem.at[q, 0])
        for dh in range(2):
            for dx in range(4):
                if dh or dx:
                    slot = 2 * lax.rem(x + 4 - dx, 4) + lax.rem(h + dh, 2)
                    arrived(W[q].at[0, slot], a_sem.at[q, dh * 4 + dx])
        for half in range(2):
            row = a_half(q, 0, half)
            send(row, a_half(q, 1, half), az_sem.at[q, 1, half], z_dev(1))
            send(row, a_half(q, 5, half), az_sem.at[q, 5, half], z_dev(-1))

    def ways(d):
        return [w for w in ((d, 4, 1), (4 + d, 7, -1)) if w[0] <= w[1]]

    def tick_a(q, d):
        for half in range(2):
            for e, last, way in ways(d):
                row = a_half(q, e, half)
                arrived(row, az_sem.at[q, e, half])
                if e < last:
                    send(row, a_half(q, e + 1, half), az_sem.at[q, e + 1, half], z_dev(way))

    def tick_b(q, d):
        for e, last, way in ways(d):
            mine = b_item(q, e, x)
            arrived(mine, bz_sem.at[q, e])
            if e < last:
                send(mine, b_item(q, e + 1, x), bz_sem.at[q, e + 1], z_dev(way))
            x_sends(q, e)

    def tick_x(q, d):
        for e in items(d):
            passed = b_item(q, e, x_at(-1))
            arrived(passed, bx_sem.at[q, e, 0])
            send(passed, passed, bx_sem.at[q, e, 2], x_dev(1))

    def items(d):
        return (0,) if d == 0 else [w[0] for w in ways(d)]

    def tick_k(q, d):
        for e in items(d):
            arrived(b_item(q, e, x_at(1)), bx_sem.at[q, e, 1])
            arrived(b_item(q, e, x_at(2)), bx_sem.at[q, e, 2])

    def exchange():
        send(i_in, i_all.at[1], i_sem.at[1], core)
        send(x_in, x_all.at[1], x_sem.at[1], core)
        for side in range(2):
            span = pl.ds(side * PIECE, PIECE)
            send(i_in, i_all.at[2 + 2 * side], i_sem.at[2 + 2 * side], across[side])
            send(x_in.at[span], x_all.at[2, span], x_sem.at[2 + 2 * side], across[side])

    def others():
        for side in range(2):
            span = pl.ds(side * PIECE, PIECE)
            got, passed = 2 + 2 * side, 3 + 2 * side
            arrived(i_all.at[got], i_sem.at[got])
            send(i_all.at[got], i_all.at[passed], i_sem.at[passed], core)
            arrived(x_all.at[2, span], x_sem.at[got])
            send(x_all.at[2, span], x_all.at[3, span], x_sem.at[passed], core)

    def ready():
        arrived(i_all.at[1], i_sem.at[1])
        arrived(x_all.at[1], x_sem.at[1])
        keep.wait()
        keep_x.wait()
        arrived(i_all.at[3], i_sem.at[3])
        arrived(i_all.at[5], i_sem.at[5])
        table = pltpu.make_async_copy(i_all, i_smem, loc_sem.at[3 + chunks])
        table.start()
        for side in range(2):
            span = pl.ds(side * PIECE, PIECE)
            arrived(x_all.at[3, span], x_sem.at[3 + 2 * side])
        table.wait()

    def products(q, group, first, store):
        terms = range(8)
        many = len(terms)
        halves = []
        for k in range(first, first + PIECE):
            table = group + 2 if group >= 2 and k >= PIECE else group
            left = i_smem[table, 0, k]
            spot, half, odd = (left >> 1) & 3, left >> 3, left & 1
            slot = jnp.where(odd == 0, 2 * spot + half, b_at(q, spot) + half)
            tall = jnp.concatenate([W[q][e, slot] for e in terms], axis=0)
            halves.append(jnp.dot(
                tall, x_all[group, k], preferred_element_type=jnp.float32
            ).astype(jnp.bfloat16))
        for k, mixed in zip(range(first, first + PIECE), halves):
            table = group + 2 if group >= 2 and k >= PIECE else group
            wide = jnp.concatenate([mixed[e * rows:(e + 1) * rows] for e in range(many)], axis=1)
            at = b_at(0, i_smem[table, 0, held + k]) + 2
            chosen = jnp.concatenate(
                [W[0][e, at + i] for e in terms for i in range(chunks)], axis=0)
            store(k, jnp.dot(wide, chosen, preferred_element_type=jnp.float32))

    def piece(q, number):
        finish(q, number // 2, (number % 2,))

    def finish(q, stage, sides):
        group = 3 - stage

        def to_part(k, value):
            part[q, stage, k] = value.astype(jnp.bfloat16)

        def to_acc(k, value):
            acc[k] = value
        for side in sides:
            products(q, group, side * PIECE, to_acc if stage % 2 else to_part)
        for side in sides:
            span = pl.ds(side * PIECE, PIECE)
            if stage == 0:
                send(part.at[q, 0, span], got_core.at[q, 0, span], red_sem.at[q, 0, side], core)
            if stage == 1:
                arrived(got_core.at[q, 0, span], red_sem.at[q, 0, side])
                part[q, 1, span] = (
                    acc[span] + got_core[q, 0, span].astype(jnp.float32)).astype(jnp.bfloat16)
                send(part.at[q, 1, span], got_y.at[q, span], red_sem.at[q, 1, side], across[side])
            if stage == 2:
                send(part.at[q, 2, span], got_core.at[q, 1, span], red_sem.at[q, 2, side], core)
            if stage == 3:
                arrived(got_core.at[q, 1, span], red_sem.at[q, 2, side])
                arrived(got_y.at[q, span], red_sem.at[q, 1, side])
                total = (acc[span] + got_core[q, 1, span].astype(jnp.float32)
                         + got_y[q, span].astype(jnp.float32))
                o_ref[span, pl.ds(q * rows, rows)] = total.astype(jnp.bfloat16)

    for name in ORDER:
        if name in ("o", "O"):
            (others if name == "o" else ready)()
            continue
        q, what, d = int(name[0]), name[1], int(name[2:] or 0)
        if what == "R":
            column_ready(q)
        if what == "r":
            row_ready(q)
            if q == 0:
                exchange()
        if what == "A":
            tick_a(q, d)
        if what == "B":
            tick_b(q, d)
        if what == "X":
            tick_x(q, d)
        if what == "K":
            tick_k(q, d)
        if what == "S":
            finish(q, d, (0, 1))
        if what == "P":
            piece(q, d)

    for made in pending:
        made.wait_send()
    for kept, index in ((head0, 0), (head1, 1)):
        @pl.when(c == index)
        def _():
            for number in range(len(kept)):
                pltpu.make_async_remote_copy(
                    src_ref=l_in.at[0, 0], dst_ref=W[0].at[0, 0], send_sem=head_sem.at[number],
                    recv_sem=a_sem.at[0, 0], device_id=core, device_id_type=MESH).wait_send()


def local(wavefunction, left_sector, right_sector, left_blocks, right_blocks):
    held, order = wavefunction.shape[:2]
    rows = order // CHUNKS
    index = jnp.concatenate([left_sector[:, 0], right_sector])
    index = jnp.pad(index[None], ((0, 7), (0, 128 - 2 * held)))
    left = left_blocks.reshape(2, CHUNKS, rows, order)
    bf16 = jnp.bfloat16
    dma = pltpu.SemaphoreType.DMA
    scratch = [
        pltpu.VMEM((8, 8 + 4 * (2 + (CHUNKS if q == 0 else 0)), rows, order), bf16)
        for q in range(CHUNKS)
    ]
    scratch += [
        pltpu.VMEM((4, held, order, order), bf16),
        pltpu.VMEM((6, 8, 128), jnp.int32),
        pltpu.SMEM((6, 8, 128), jnp.int32),
        pltpu.VMEM((order, order), bf16),
        pltpu.VMEM((CHUNKS, 3, held, rows, order), bf16),
        pltpu.VMEM((held, rows, order), jnp.float32),
        pltpu.VMEM((CHUNKS, 2, held, rows, order), bf16),
        pltpu.VMEM((CHUNKS, held, rows, order), bf16),
        dma((12 + 60 * CHUNKS,)),
        dma((15 * CHUNKS,)),
        dma((CHUNKS, 8)),
        dma((CHUNKS, 2)),
        dma((CHUNKS, 8, 2)),
        dma((CHUNKS, 8)),
        dma((CHUNKS, 8, 3)),
        dma((6,)),
        dma((6,)),
        dma((CHUNKS, 3, 2)),
        dma((CHUNKS + 4,)),
    ]
    vmem, anywhere = pl.BlockSpec(memory_space=pltpu.VMEM), pl.BlockSpec(memory_space=pl.ANY)
    return pl.pallas_call(
        kernel,
        out_shape=jax.ShapeDtypeStruct(wavefunction.shape, wavefunction.dtype),
        in_specs=[anywhere, vmem, anywhere, anywhere],
        out_specs=vmem,
        scratch_shapes=scratch,
        compiler_params=pltpu.CompilerParams(
            collective_id=0, has_side_effects=True, vmem_limit_bytes=56 * 1024 * 1024),
        name="terms",
    )(wavefunction, index, left, right_blocks)


def solution(mesh):
    placed = (
        P(("term", "sector"), None, None),
        P(("term", "sector"), None),
        P(("term", "sector")),
        P("term", "sector", None, None),
        P("term", None, None, None),
    )
    return jax.shard_map(
        local,
        mesh=mesh,
        in_specs=placed,
        out_specs=P(("term", "sector"), None, None),
        check_vma=False,
    )
```

```python
import functools

import jax
import jax.numpy as jnp
from jax import lax
from jax.experimental import pallas as pl
from jax.experimental.pallas import tpu as pltpu
from jax.sharding import PartitionSpec as P

CHUNKS = 2
PIECE = 8
MESH = pl.DeviceIdType.MESH
ORDER = (
    "0R", "1R", "0r", "0B1", "0X0", "0A1", "0B2", "0X1", "0A2", "1r", "0B3", "0X2", "0B4", "o",
    "0A3", "0X3", "1B1", "1X0", "1A1", "0X4", "1B2", "1X1", "1A2", "1B3", "0A4", "0K0", "0K1",
    "0K2", "0K3", "0K4", "O", "0P0", "1X2", "1A3", "0P1", "0P2", "1B4", "0P3", "1X3", "0P4",
    "1X4", "0P5", "0P6", "0P7", "1A4", "1K0", "1K1", "1K2", "1K3", "1K4", "1P0", "1P1", "1P2",
    "1P3", "1P4", "1P5", "1P6", "1P7",
)


def kernel(x_in, i_in, l_in, r_in, o_ref, *scratch):
    chunks = CHUNKS
    W = scratch[:chunks]
    (x_all, i_all, i_smem, r_own, part, acc, got_core, got_y,
     send_sem, head_sem, a_sem, b_sem, az_sem, bz_sem, bx_sem, x_sem, i_sem, red_sem,
     loc_sem) = scratch[chunks:]
    held, order = x_in.shape[0], x_in.shape[1]
    rows = order // chunks
    term, sector = lax.axis_index("term"), lax.axis_index("sector")
    p, z = term // 8, lax.rem(term, 8)
    h, x, c = sector // 8, lax.rem(sector // 2, 4), lax.rem(sector, 2)
    turn = 1 - 2 * c
    core = (term, sector + turn)
    across = ((lax.rem(term + 8, 16), sector),
              (lax.rem(term + 8, 16), lax.rem(sector + 8, 16)))

    def z_at(k):
        return lax.rem(z + 16 + k * turn, 8)

    def x_at(k):
        return lax.rem(x + 8 + k * turn, 4)

    def z_dev(k):
        return (p * 8 + z_at(k), sector)

    def x_dev(k):
        return (term, h * 8 + x_at(k) * 2 + c)

    def plane(dh, dx, core_index):
        return (term, lax.rem(h + dh, 2) * 8 + lax.rem(x + dx, 4) * 2 + core_index)

    def width(q):
        return 2 + (chunks if q == 0 else 0)

    def b_at(q, xx):
        return 8 + xx * width(q)

    def a_half(q, e, half):
        return W[q].at[e, pl.ds(4 * half, 4)]

    def b_item(q, e, xx):
        return W[q].at[e, pl.ds(b_at(q, xx), width(q))]

    right_own = pltpu.make_async_copy(r_in.at[c, x], r_own, loc_sem.at[0])
    right_own.start()
    keep = pltpu.make_async_copy(i_in, i_all.at[0], loc_sem.at[1])
    keep.start()
    keep_x = pltpu.make_async_copy(x_in, x_all.at[0], loc_sem.at[2])
    keep_x.start()

    barrier = pltpu.get_barrier_semaphore()
    peers = [*across, z_dev(1), z_dev(-1), core]
    for dh in range(2):
        for dx in range(4):
            if dh or dx:
                peers += [plane(dh, dx, 0), plane(dh, dx, 1)]
    for peer in peers:
        pl.semaphore_signal(barrier, inc=1, device_id=peer, device_id_type=MESH)

    right_own.wait()
    turned = r_own[...].T
    for i in range(chunks):
        W[0][0, b_at(0, x) + 2 + i] = turned[i * rows:(i + 1) * rows]

    pl.semaphore_wait(barrier, len(peers))

    pending, head0, head1 = [], [], []

    def send(src, dst, recv, device, kept=None):
        kept, sems = (pending, send_sem) if kept is None else (kept, head_sem)
        made = pltpu.make_async_remote_copy(
            src_ref=src, dst_ref=dst, send_sem=sems.at[len(kept)], recv_sem=recv,
            device_id=device, device_id_type=MESH)
        made.start()
        kept.append(made)

    def arrived(dst, recv):
        pltpu.make_async_remote_copy(
            src_ref=dst, dst_ref=dst, send_sem=send_sem.at[0], recv_sem=recv,
            device_id=core, device_id_type=MESH).wait_recv()

    def own_copy(q):
        slot = jnp.where(c == 0, 2 * x + h, b_at(q, x) + h)
        return pltpu.make_async_copy(l_in.at[c, q], W[q].at[0, slot], loc_sem.at[3 + q])

    for q in range(chunks):
        own_copy(q).start()

        @pl.when(c == 1)
        def _():
            slot = b_at(q, x) + h
            send(l_in.at[0, q], W[q].at[0, slot], b_sem.at[q, 0], core, head1)
            for j in range(2):
                send(l_in.at[j, q], W[q].at[0, slot], b_sem.at[q, 1], plane(1, 0, j), head1)

        @pl.when(c == 0)
        def _():
            slot = 2 * x + h
            for dh, dx in ((1, 2), (0, 2), (1, 1), (1, 3), (1, 0), (0, 1), (0, 3)):
                for j in range(2):
                    send(l_in.at[j, q], W[q].at[0, slot], a_sem.at[q, dh * 4 + dx],
                         plane(dh, dx, j), head0)
            send(l_in.at[1, q], W[q].at[0, slot], a_sem.at[q, 0], core, head0)

    def x_sends(q, e):
        mine = b_item(q, e, x)
        send(mine, mine, bx_sem.at[q, e, 0], x_dev(1))
        send(mine, mine, bx_sem.at[q, e, 1], x_dev(-1))

    def column_ready(q):
        @pl.when(c == 0)
        def _():
            arrived(W[q].at[0, b_at(q, x) + h], b_sem.at[q, 0])

        @pl.when(c == 1)
        def _():
            own_copy(q).wait()
        arrived(W[q].at[0, b_at(q, x) + 1 - h], b_sem.at[q, 1])
        mine = b_item(q, 0, x)
        send(mine, b_item(q, 1, x), bz_sem.at[q, 1], z_dev(1))
        send(mine, b_item(q, 5, x), bz_sem.at[q, 5], z_dev(-1))
        x_sends(q, 0)

    def row_ready(q):
        @pl.when(c == 0)
        def _():
            own_copy(q).wait()

        @pl.when(c == 1)
        def _():
            arrived(W[q].at[0, 2 * x + h], a_sem.at[q, 0])
        for dh in range(2):
            for dx in range(4):
                if dh or dx:
                    slot = 2 * lax.rem(x + 4 - dx, 4) + lax.rem(h + dh, 2)
                    arrived(W[q].at[0, slot], a_sem.at[q, dh * 4 + dx])
        for half in range(2):
            row = a_half(q, 0, half)
            send(row, a_half(q, 1, half), az_sem.at[q, 1, half], z_dev(1))
            send(row, a_half(q, 5, half), az_sem.at[q, 5, half], z_dev(-1))

    def ways(d):
        return [w for w in ((d, 4, 1), (4 + d, 7, -1)) if w[0] <= w[1]]

    def tick_a(q, d):
        for half in range(2):
            for e, last, way in ways(d):
                row = a_half(q, e, half)
                arrived(row, az_sem.at[q, e, half])
                if e < last:
                    send(row, a_half(q, e + 1, half), az_sem.at[q, e + 1, half], z_dev(way))

    def tick_b(q, d):
        for e, last, way in ways(d):
            mine = b_item(q, e, x)
            arrived(mine, bz_sem.at[q, e])
            if e < last:
                send(mine, b_item(q, e + 1, x), bz_sem.at[q, e + 1], z_dev(way))
            x_sends(q, e)

    def tick_x(q, d):
        for e in items(d):
            passed = b_item(q, e, x_at(-1))
            arrived(passed, bx_sem.at[q, e, 0])
            send(passed, passed, bx_sem.at[q, e, 2], x_dev(1))

    def items(d):
        return (0,) if d == 0 else [w[0] for w in ways(d)]

    def tick_k(q, d):
        for e in items(d):
            arrived(b_item(q, e, x_at(1)), bx_sem.at[q, e, 1])
            arrived(b_item(q, e, x_at(2)), bx_sem.at[q, e, 2])

    def exchange():
        send(i_in, i_all.at[1], i_sem.at[1], core)
        send(x_in, x_all.at[1], x_sem.at[1], core)
        for side in range(2):
            span = pl.ds(side * PIECE, PIECE)
            send(i_in, i_all.at[2 + 2 * side], i_sem.at[2 + 2 * side], across[side])
            send(x_in.at[span], x_all.at[2, span], x_sem.at[2 + 2 * side], across[side])

    def others():
        for side in range(2):
            span = pl.ds(side * PIECE, PIECE)
            got, passed = 2 + 2 * side, 3 + 2 * side
            arrived(i_all.at[got], i_sem.at[got])
            send(i_all.at[got], i_all.at[passed], i_sem.at[passed], core)
            arrived(x_all.at[2, span], x_sem.at[got])
            send(x_all.at[2, span], x_all.at[3, span], x_sem.at[passed], core)

    def ready():
        arrived(i_all.at[1], i_sem.at[1])
        arrived(x_all.at[1], x_sem.at[1])
        keep.wait()
        keep_x.wait()
        arrived(i_all.at[3], i_sem.at[3])
        arrived(i_all.at[5], i_sem.at[5])
        table = pltpu.make_async_copy(i_all, i_smem, loc_sem.at[3 + chunks])
        table.start()
        for side in range(2):
            span = pl.ds(side * PIECE, PIECE)
            arrived(x_all.at[3, span], x_sem.at[3 + 2 * side])
        table.wait()

    def products(q, group, first, store):
        terms = range(8)
        many = len(terms)
        halves = []
        for k in range(first, first + PIECE):
            table = group + 2 if group >= 2 and k >= PIECE else group
            left = i_smem[table, 0, k]
            spot, half, odd = (left >> 1) & 3, left >> 3, left & 1
            slot = jnp.where(odd == 0, 2 * spot + half, b_at(q, spot) + half)
            tall = jnp.concatenate([W[q][e, slot] for e in terms], axis=0)
            halves.append(jnp.dot(
                tall, x_all[group, k], preferred_element_type=jnp.float32
            ).astype(jnp.bfloat16))
        for k, mixed in zip(range(first, first + PIECE), halves):
            table = group + 2 if group >= 2 and k >= PIECE else group
            wide = jnp.concatenate([mixed[e * rows:(e + 1) * rows] for e in range(many)], axis=1)
            at = b_at(0, i_smem[table, 0, held + k]) + 2
            chosen = jnp.concatenate(
                [W[0][e, at + i] for e in terms for i in range(chunks)], axis=0)
            store(k, jnp.dot(wide, chosen, preferred_element_type=jnp.float32))

    def piece(q, number):
        finish(q, number // 2, (number % 2,))

    def finish(q, stage, sides):
        group = 3 - stage

        def to_part(k, value):
            part[q, stage, k] = value.astype(jnp.bfloat16)

        def to_acc(k, value):
            acc[k] = value
        for side in sides:
            products(q, group, side * PIECE, to_acc if stage % 2 else to_part)
        for side in sides:
            span = pl.ds(side * PIECE, PIECE)
            if stage == 0:
                send(part.at[q, 0, span], got_core.at[q, 0, span], red_sem.at[q, 0, side], core)
            if stage == 1:
                arrived(got_core.at[q, 0, span], red_sem.at[q, 0, side])
                part[q, 1, span] = (
                    acc[span] + got_core[q, 0, span].astype(jnp.float32)).astype(jnp.bfloat16)
                send(part.at[q, 1, span], got_y.at[q, span], red_sem.at[q, 1, side], across[side])
            if stage == 2:
                send(part.at[q, 2, span], got_core.at[q, 1, span], red_sem.at[q, 2, side], core)
            if stage == 3:
                arrived(got_core.at[q, 1, span], red_sem.at[q, 2, side])
                arrived(got_y.at[q, span], red_sem.at[q, 1, side])
                total = (acc[span] + got_core[q, 1, span].astype(jnp.float32)
                         + got_y[q, span].astype(jnp.float32))
                o_ref[span, pl.ds(q * rows, rows)] = total.astype(jnp.bfloat16)

    for name in ORDER:
        if name in ("o", "O"):
            (others if name == "o" else ready)()
            continue
        q, what, d = int(name[0]), name[1], int(name[2:] or 0)
        if what == "R":
            column_ready(q)
        if what == "r":
            row_ready(q)
            if q == 0:
                exchange()
        if what == "A":
            tick_a(q, d)
        if what == "B":
            tick_b(q, d)
        if what == "X":
            tick_x(q, d)
        if what == "K":
            tick_k(q, d)
        if what == "S":
            finish(q, d, (0, 1))
        if what == "P":
            piece(q, d)

    for made in pending:
        made.wait_send()
    for kept, index in ((head0, 0), (head1, 1)):
        @pl.when(c == index)
        def _():
            for number in range(len(kept)):
                pltpu.make_async_remote_copy(
                    src_ref=l_in.at[0, 0], dst_ref=W[0].at[0, 0], send_sem=head_sem.at[number],
                    recv_sem=a_sem.at[0, 0], device_id=core, device_id_type=MESH).wait_send()


def local(wavefunction, left_sector, right_sector, left_blocks, right_blocks):
    held, order = wavefunction.shape[:2]
    rows = order // CHUNKS
    index = jnp.concatenate([left_sector[:, 0], right_sector])
    index = jnp.pad(index[None], ((0, 7), (0, 128 - 2 * held)))
    left = left_blocks.reshape(2, CHUNKS, rows, order)
    bf16 = jnp.bfloat16
    dma = pltpu.SemaphoreType.DMA
    scratch = [
        pltpu.VMEM((8, 8 + 4 * (2 + (CHUNKS if q == 0 else 0)), rows, order), bf16)
        for q in range(CHUNKS)
    ]
    scratch += [
        pltpu.VMEM((4, held, order, order), bf16),
        pltpu.VMEM((6, 8, 128), jnp.int32),
        pltpu.SMEM((6, 8, 128), jnp.int32),
        pltpu.VMEM((order, order), bf16),
        pltpu.VMEM((CHUNKS, 3, held, rows, order), bf16),
        pltpu.VMEM((held, rows, order), jnp.float32),
        pltpu.VMEM((CHUNKS, 2, held, rows, order), bf16),
        pltpu.VMEM((CHUNKS, held, rows, order), bf16),
        dma((12 + 60 * CHUNKS,)),
        dma((15 * CHUNKS,)),
        dma((CHUNKS, 8)),
        dma((CHUNKS, 2)),
        dma((CHUNKS, 8, 2)),
        dma((CHUNKS, 8)),
        dma((CHUNKS, 8, 3)),
        dma((6,)),
        dma((6,)),
        dma((CHUNKS, 3, 2)),
        dma((CHUNKS + 4,)),
    ]
    vmem, anywhere = pl.BlockSpec(memory_space=pltpu.VMEM), pl.BlockSpec(memory_space=pl.ANY)
    return pl.pallas_call(
        kernel,
        out_shape=jax.ShapeDtypeStruct(wavefunction.shape, wavefunction.dtype),
        in_specs=[anywhere, vmem, anywhere, anywhere],
        out_specs=vmem,
        scratch_shapes=scratch,
        compiler_params=pltpu.CompilerParams(
            collective_id=0, has_side_effects=True, vmem_limit_bytes=56 * 1024 * 1024),
        name="terms",
    )(wavefunction, index, left, right_blocks)


def solution(mesh):
    placed = (
        P(("term", "sector"), None, None),
        P(("term", "sector"), None),
        P(("term", "sector")),
        P("term", "sector", None, None),
        P("term", None, None, None),
    )
    return jax.shard_map(
        local,
        mesh=mesh,
        in_specs=placed,
        out_specs=P(("term", "sector"), None, None),
        check_vma=False,
    )
```
